32 devices in a mesh: row: 8 (over z, y), col: 4 (over x, core).
Axes of the slice: x: 2, y: 2, z: 4, core: 2. Of those that a mesh axis runs over, the one named last changes fastest.
Arguments:
- points: bfloat16 [4096, 768], P(('row', 'col')), may hold values from -100 to 100
- labels: int32 [4096], P(('row', 'col')), may hold values from 0 to 99
- projection: bfloat16 [256, 768], replicated, may hold values from -0.015625 to 0.015625
Outputs:
- gradient: float32 [256, 768], P('row', 'col')
- class_prob: float32 [4096], P(('row', 'col'))
The draws below stay inside these ranges and needn't reach their ends.
All inputs are finite; a program needn't handle non-finite values.
Results may differ from the reference program's by a relative error of at most 0.00081.
Values may be sent and summed in bfloat16 or wider, within the bound.
No kernel may reach another device: no remote copies, remote signals or barrier semaphores. Data moves between devices by JAX's collectives and lax.ppermute only.
A program may use at most 64 MiB of HBM per device.

```python
import jax
import jax.numpy as jnp
from jax import lax

D = 768
E = 256
CLASSES = 100
NPTS = 4096


def shared_labels(key):
    return jax.random.randint(jax.random.fold_in(key, 1), (NPTS,), 0, CLASSES)


def draw_labels(key, part):
    return shared_labels(key).astype(jnp.int32)


def draw_points(key, part):
    classes_of = shared_labels(key)
    centers = jnp.clip(jax.random.normal(jax.random.fold_in(key, 2), (CLASSES, D), jnp.float32), -3.0, 3.0)
    noise = jnp.clip(jax.random.normal(jax.random.fold_in(key, 3), (NPTS, D), jnp.float32), -4.0, 4.0)
    values = centers[classes_of] + noise
    return values.astype(jnp.bfloat16)


def normal_values(rng, dims, width, most, kind=jnp.bfloat16):
    values = width * jax.random.normal(rng, dims, jnp.float32)
    return jnp.clip(values, min=-most, max=most).astype(kind)


def setup_inputs(seed: int = 0) -> dict:
    keys = jax.random.split(jax.random.key(seed), 4)
    points = draw_points(jax.random.fold_in(keys[3], 71), 0)
    labels = draw_labels(jax.random.fold_in(keys[3], 71), 0)
    projection = normal_values(keys[2], (E, D), (4 * D * E // 5) ** -0.5, 0.015625)
    return dict(points=points, labels=labels, projection=projection)


def reference(points, labels, projection):
    proj = jnp.dot(points, projection.T, preferred_element_type=jnp.float32).astype(jnp.bfloat16)
    proj_f = proj.astype(jnp.float32)
    sqnorm = jnp.sum(proj_f * proj_f, axis=1)
    total_pts = points.shape[0]
    blocksz = min(512, total_pts)
    count = total_pts // blocksz
    position = jnp.arange(total_pts, dtype=jnp.int32)
    block_proj = proj.reshape(count, blocksz, proj.shape[1])
    block_norm = sqnorm.reshape(count, blocksz)
    block_pos = position.reshape(count, blocksz)
    block_lab = labels.reshape(count, blocksz)

    def scores(rows_proj, rows_norm, rows_pos):
        inner = jnp.dot(rows_proj, proj.T, preferred_element_type=jnp.float32)
        value = -(rows_norm[:, None] + sqnorm[None, :] - 2.0 * inner)
        return jnp.where(rows_pos[:, None] == position[None, :], -jnp.inf, value)

    def first_pass(items):
        rows_proj, rows_norm, rows_pos, rows_lab = items
        value = scores(rows_proj, rows_norm, rows_pos)
        top = jnp.max(value, axis=1)
        expo = jnp.exp(value - top[:, None])
        match = rows_lab[:, None] == labels[None, :]
        return top, jnp.sum(expo, axis=1), jnp.sum(jnp.where(match, expo, 0.0), axis=1)

    top, total, same = lax.map(first_pass, (block_proj, block_norm, block_pos, block_lab))
    class_prob = same / total

    def second_pass(carry, items):
        col_sum, wtz = carry
        rows_proj, rows_norm, rows_pos, rows_lab, rows_top, rows_total, rows_prob = items
        value = scores(rows_proj, rows_norm, rows_pos)
        pick = jnp.exp(value - rows_top[:, None]) / rows_total[:, None]
        match = (rows_lab[:, None] == labels[None, :]).astype(jnp.float32)
        weight = (pick * (rows_prob[:, None] - match)).astype(jnp.bfloat16)
        weight_f = weight.astype(jnp.float32)
        row_sum = jnp.sum(weight_f, axis=1)
        pull_rows = rows_proj.astype(jnp.float32) * row_sum[:, None] - jnp.dot(weight, proj, preferred_element_type=jnp.float32)
        col_sum = col_sum + jnp.sum(weight_f, axis=0)
        wtz = wtz + jnp.dot(weight.T, rows_proj, preferred_element_type=jnp.float32)
        return (col_sum, wtz), pull_rows

    start = (jnp.zeros((total_pts,), jnp.float32), jnp.zeros((total_pts, proj.shape[1]), jnp.float32))
    (col_sum, wtz), pull_rows = lax.scan(second_pass, start, (block_proj, block_norm, block_pos, block_lab, top, total, class_prob))
    pull = pull_rows.reshape(total_pts, proj.shape[1]) + proj_f * col_sum[:, None] - wtz
    pull_high = pull.astype(jnp.bfloat16)
    pull_low = (pull - pull_high.astype(jnp.float32)).astype(jnp.bfloat16)
    gradient = jnp.dot(pull_high.T, points, preferred_element_type=jnp.float32)
    gradient = gradient + jnp.dot(pull_low.T, points, preferred_element_type=jnp.float32)
    return 2.0 * gradient, class_prob.reshape(total_pts)
```

```python
import functools

import jax
import jax.numpy as jnp
from jax import lax
from jax.experimental import pallas as pl
from jax.experimental.pallas import tpu as pltpu
from jax.sharding import PartitionSpec as P

AXES = ("row", "col")
F32 = jnp.float32
BF16 = jnp.bfloat16
PAD = 16


def dot(lhs, rhs, dims):
    return lax.dot_general(lhs, rhs, (dims, ((), ())), preferred_element_type=F32)


def call(body, outs, args, flops=1 << 28):
    bytes_moved = sum(a.size * a.dtype.itemsize for a in list(args) + list(outs))
    return pl.pallas_call(
        body,
        out_shape=outs,
        in_specs=[pl.BlockSpec(memory_space=pltpu.VMEM)] * len(args),
        out_specs=[pl.BlockSpec(memory_space=pltpu.VMEM)] * len(outs),
        cost_estimate=pl.CostEstimate(flops=flops, bytes_accessed=bytes_moved, transcendentals=0),
    )(*args)


def embed_body(points_ref, labels_ref, projection_ref, out_ref):
    width, count = projection_ref.shape[0], points_ref.shape[0]
    out_ref[:width] = dot(projection_ref[...], points_ref[...], ((1,), (1,))).astype(BF16)
    out_ref[width:] = jnp.broadcast_to(labels_ref[...].astype(F32), (PAD, count)).astype(BF16)


def stats_body(n_first, n_second, *refs):
    first, second = refs[:n_first], refs[n_first : n_first + n_second]
    expo_ref, stat_ref = refs[n_first + n_second :]
    width, count = first[0].shape[0] - PAD, first[0].shape[1]
    proj, norm, lab = [], [], []
    for ref in second:
        block = ref[:width].T
        proj.append(block)
        norm.append(jnp.sum(jnp.square(block.astype(F32)), axis=1, keepdims=True))
        lab.append(jnp.broadcast_to(ref[width : width + 1].astype(F32), (count, count)).T)
    proj = jnp.concatenate(proj, axis=0)
    norm = jnp.broadcast_to(jnp.concatenate(norm, axis=0), (n_second * count, count))
    lab = jnp.concatenate(lab, axis=0)
    for a, ref in enumerate(first):
        block = ref[:width]
        own_norm = jnp.sum(jnp.square(block.astype(F32)), axis=0, keepdims=True)
        value = 2.0 * dot(proj, block, ((1,), (0,))) - (own_norm + norm)
        if a == 0:
            shape = (n_second * count, count)
            same_point = lax.broadcasted_iota(jnp.int32, shape, 0) == lax.broadcasted_iota(jnp.int32, shape, 1)
            value = jnp.where(same_point, -jnp.inf, value)
        top = jnp.max(value, axis=0, keepdims=True)
        expo = jnp.exp(value - top)
        match = lab == ref[width : width + 1].astype(F32)
        total = jnp.sum(expo, axis=0, keepdims=True)
        same = jnp.sum(jnp.where(match, expo, 0.0), axis=0, keepdims=True)
        expo_ref[:, a * count : (a + 1) * count] = jnp.where(match, -expo, expo)
        for s, stat in enumerate((top, total, same)):
            stat_ref[s * n_first + a : s * n_first + a + 1] = stat


def pull_body(n_first, n_second, *refs):
    stats = refs[:n_first]
    refs = refs[n_first:]
    first, second = refs[:n_first], refs[n_first : n_first + n_second]
    expo_ref, high_ref, low_ref, prob_ref, weight_ref = refs[n_first + n_second :]
    width, count = first[0].shape[0] - PAD, first[0].shape[1]

    def emit(value, start, size):
        high = value.astype(BF16)
        high_ref[:, start : start + size] = high
        low_ref[:, start : start + size] = (value - high.astype(F32)).astype(BF16)

    proj_first = jnp.concatenate([ref[:width] for ref in first], axis=1)
    proj_second = jnp.concatenate([ref[:width] for ref in second], axis=1)
    row_sum = []
    for a in range(n_first):
        def stat(s, m):
            at = s * n_first + (a ^ m)
            return stats[m][at : at + 1]

        tops = [stat(0, m) for m in range(n_first)]
        top = functools.reduce(jnp.maximum, tops)
        factor = [jnp.exp(t - top) for t in tops]
        total = sum(stat(1, m) * factor[m] for m in range(n_first))
        same = sum(stat(2, m) * factor[m] for m in range(n_first))
        prob = same / total
        if a == 0:
            prob_ref[...] = jnp.broadcast_to(prob, prob_ref.shape)
        scale = factor[0] / total
        expo = expo_ref[:, a * count : (a + 1) * count]
        weight = (expo * jnp.where(expo < 0.0, scale * (1.0 - prob), scale * prob)).astype(BF16)
        row_sum.append(jnp.sum(weight.astype(F32), axis=0, keepdims=True))
        weight_ref[:, a * count : (a + 1) * count] = weight
    weight = weight_ref[...]
    row_sum = jnp.concatenate(row_sum, axis=1)
    col_sum = dot(jnp.ones((8, n_first * count), BF16), weight, ((1,), (1,)))[:1]
    emit(
        proj_first.astype(F32) * row_sum - dot(proj_second, weight, ((1,), (0,))),
        0,
        n_first * count,
    )
    emit(
        proj_second.astype(F32) * col_sum - dot(proj_first, weight, ((1,), (1,))),
        n_first * count,
        n_second * count,
    )


def pack_chunk(value, rows, cols, r, q):
    tile = value[r * rows : (r + 1) * rows]
    base = q * cols
    if base % 128 == 0:
        wide, rest = tile[:, base : base + 128], tile[:, base + 128 : base + 192]
    else:
        wide, rest = tile[:, base + 64 : base + 192], tile[:, base : base + 64]
    half = rows // 2
    return jnp.concatenate([wide, jnp.concatenate([rest[:half], rest[half:]], axis=1)], axis=0)


def gradient_body(n_blocks, row_devs, col_devs, *refs):
    pos_ref, high_ref, low_ref = refs[:3]
    points = refs[3 : 3 + n_blocks]
    mine_ref, other_ref = refs[3 + n_blocks :]
    count = points[0].shape[0]
    feats = jnp.concatenate([ref[...] for ref in points], axis=0)
    value = dot(high_ref[...], feats, ((1,), (0,))) + dot(low_ref[...], feats, ((1,), (0,)))
    rows, cols = value.shape[0] // row_devs, value.shape[1] // col_devs
    size = rows * cols // 128
    pair, core = pos_ref[0], pos_ref[1]
    for r in range(row_devs):
        for x in range(col_devs // 2):
            pieces = [pack_chunk(value, rows, cols, r, 2 * x + c) for c in range(2)]
            slot = (r * (col_devs // 2) + x) ^ pair
            at = pl.ds(pl.multiple_of(slot * size, size), size)
            mine_ref[at] = jnp.where(core == 0, pieces[0], pieces[1])
            other_ref[at] = jnp.where(core == 0, pieces[1], pieces[0])


def gradient_call(pos, high, low, points, row_devs, col_devs):
    width, feats = high.shape[0], points[0].shape[1]
    half = jax.ShapeDtypeStruct((width * feats // 2 // 128, 128), F32)
    args = [high, low, *points]
    return pl.pallas_call(
        functools.partial(gradient_body, len(points), row_devs, col_devs),
        out_shape=[half, half],
        in_specs=[pl.BlockSpec(memory_space=pltpu.SMEM)]
        + [pl.BlockSpec(memory_space=pltpu.VMEM)] * len(args),
        out_specs=[pl.BlockSpec(memory_space=pltpu.VMEM)] * 2,
        cost_estimate=pl.CostEstimate(flops=1 << 30, bytes_accessed=1 << 22, transcendentals=0),
    )(pos, *args)


def fold_body(mine_ref, other_ref, *outs):
    size = outs[0].shape[0]
    for k, out in enumerate(outs):
        at = pl.ds(k * size, size)
        out[...] = mine_ref[at] + other_ref[at]


def add_body(*refs):
    *ins, out = refs
    out[...] = sum(ref[...] for ref in ins)


def finish_body(odd_ref, *refs):
    *ins, out = refs
    value = 2.0 * sum(ref[...] for ref in ins)
    rows = out.shape[0]
    half = rows // 2
    wide, rest = value[:rows], value[rows:]
    rest = jnp.concatenate([rest[:, :64], rest[:, 64:]], axis=0)
    even = jnp.concatenate([wide, rest], axis=1)
    odd = jnp.concatenate([rest, wide], axis=1)
    out[...] = jnp.where(odd_ref[0] == 1, odd, even)


def shards(points, labels, projection):
    row_devs, col_devs = lax.axis_size("row"), lax.axis_size("col")
    devices = row_devs * col_devs
    assert row_devs & (row_devs - 1) == 0 and col_devs & (col_devs - 1) == 0 and col_devs >= 2
    row_pos, col_pos = lax.axis_index("row"), lax.axis_index("col")
    count, dims = points.shape
    width = projection.shape[0]

    def swap(value, mask):
        return lax.ppermute(value, AXES, [(d, d ^ mask) for d in range(devices)])

    first_masks = range(0, 2 * col_devs, 2)
    outer_masks = range(0, devices, 2 * col_devs)
    n_first, n_second = len(first_masks), 2 * len(outer_masks)

    def gather(own):
        outer = [own] + [swap(own, m) for m in outer_masks[1:]]
        first = [own] + [swap(own, m) for m in first_masks[1:]]
        second = [part for value in outer for part in (value, swap(value, 1))]
        return first, second

    message = jax.ShapeDtypeStruct((width + PAD, count), BF16)
    own = call(embed_body, [message], [points, labels[None, :], projection], 1 << 26)[0]
    first, second = gather(own)
    pairs = (n_second * count, n_first * count)
    expo, stat = call(
        functools.partial(stats_body, n_first, n_second),
        [jax.ShapeDtypeStruct(pairs, F32), jax.ShapeDtypeStruct((-(-3 * n_first // 8) * 8, count), F32)],
        [*first, *second],
    )
    points_first, points_second = gather(points)
    stats = [stat] + [swap(stat, m) for m in first_masks[1:]]
    halves = jax.ShapeDtypeStruct((width, (n_first + n_second) * count), BF16)
    args = [*stats, *first, *second, expo]
    high, low, prob = pl.pallas_call(
        functools.partial(pull_body, n_first, n_second),
        out_shape=[halves, halves, jax.ShapeDtypeStruct((8, count), F32)],
        in_specs=[pl.BlockSpec(memory_space=pltpu.VMEM)] * len(args),
        out_specs=[pl.BlockSpec(memory_space=pltpu.VMEM)] * 3,
        scratch_shapes=[pltpu.VMEM(pairs, BF16)],
        cost_estimate=pl.CostEstimate(flops=1 << 29, bytes_accessed=1 << 23, transcendentals=0),
    )(*args)
    own_prob = prob[0]
    rows, cols = width // row_devs, dims // col_devs
    feats = [*points_first, *points_second]
    if cols % 192 or rows % 16 or devices > 64:
        value = sum(dot(half, jnp.concatenate(feats, axis=0), ((1,), (0,))) for half in (high, low))
        value = lax.psum_scatter(value, "row", scatter_dimension=0, tiled=True)
        return 2.0 * lax.psum_scatter(value, "col", scatter_dimension=1, tiled=True), own_prob
    index = row_pos * col_devs + col_pos
    pos = jnp.stack([index // 2, index % 2]).astype(jnp.int32)
    mine, other = gradient_call(pos, high, low, feats, row_devs, col_devs)
    received = swap(other, 1)
    outer = len(outer_masks)
    size = rows * cols // 128
    chips = devices // 2
    parts = call(fold_body_for(n_first, outer, size), [jax.ShapeDtypeStruct((outer * size, 128), F32)] * n_first, [mine, received], 1 << 20)
    got = [parts[0]] + [swap(part, m) for part, m in zip(parts[1:], first_masks[1:])]
    parts = call(split_body_for(outer, size), [jax.ShapeDtypeStruct((size, 128), F32)] * outer, got, 1 << 20)
    got = [parts[0]] + [swap(part, m) for part, m in zip(parts[1:], outer_masks[1:])]
    odd = (col_pos % 2).astype(jnp.int32)[None]
    gradient = pl.pallas_call(
        finish_body,
        out_shape=jax.ShapeDtypeStruct((rows, cols), F32),
        in_specs=[pl.BlockSpec(memory_space=pltpu.SMEM)] + [pl.BlockSpec(memory_space=pltpu.VMEM)] * outer,
        out_specs=pl.BlockSpec(memory_space=pltpu.VMEM),
    )(odd, *got)
    return gradient, own_prob


def fold_body_for(n_first, outer, size):
    def body(mine_ref, other_ref, *outs):
        for m, out in enumerate(outs):
            for o in range(outer):
                at = pl.ds((o * n_first + m) * size, size)
                out[o * size : (o + 1) * size] = mine_ref[at] + other_ref[at]

    return body


def split_body_for(outer, size):
    def body(*refs):
        ins, outs = refs[:-outer], refs[-outer:]
        for o, out in enumerate(outs):
            out[...] = sum(ref[o * size : (o + 1) * size] for ref in ins)

    return body


def solution(mesh):
    in_specs = (P(AXES, None), P(AXES), P())
    out_specs = (P("row", "col"), P(AXES))
    return jax.shard_map(shards, mesh=mesh, in_specs=in_specs, out_specs=out_specs, check_vma=False)
```
